256 devices in a mesh: layer: 2 (over x_lo), row: 32 (over z, y), col: 4 (over x_hi, core).
Axes of the slice: x: 4 (x_hi: 2, x_lo: 2; x = x_hi * 2 + x_lo), y: 4, z: 8, core: 2. Of those that a mesh axis runs over, the one named last changes fastest.
Arguments:
- rhs_root: float32 [16384, 128], P('col'), may hold values from -6 to 6
- rhs_child: float32 [2, 8192, 128], P('layer', 'col'), may hold values from -6 to 6
- rhs_leaf: float32 [4, 4096, 128], P('layer', 'col'), may hold values from -6 to 6
- root_inv: bfloat16 [16384, 16384], P('row', 'col'), may hold values from -0.046875 to 0.046875
- child_inv: bfloat16 [2, 8192, 8192], P('layer', 'row', 'col'), may hold values from -0.0625 to 0.0625
- leaf_inv: bfloat16 [4, 4096, 4096], P('layer', 'row', 'col'), may hold values from -0.09375 to 0.09375
- leaf_to_child: bfloat16 [4, 8192, 4096], P('layer', 'col', 'row'), may hold values from -0.0625 to 0.0625
- leaf_to_root: bfloat16 [4, 16384, 4096], P('layer', 'col', 'row'), may hold values from -0.03125 to 0.03125
- child_to_root: bfloat16 [2, 16384, 8192], P('layer', 'col', 'row'), may hold values from -0.03125 to 0.03125
Outputs:
- x_root: float32 [16384, 128], P('col')
- x_child: float32 [2, 8192, 128], P('layer', 'col')
- x_leaf: float32 [4, 4096, 128], P('layer', 'col')
- y_root: float32 [16384, 128], P('row')
The draws below stay inside these ranges and needn't reach their ends.
All inputs are finite; a program needn't handle non-finite values.
Results may differ from the reference program's by a relative error of at most 0.008.
Values sent between devices are 32-bit elements; how exact they have to be, the bound alone decides.
No kernel may reach another device: no remote copies, remote signals or barrier semaphores. Data moves between devices by JAX's collectives and lax.ppermute only.
A program may use at most 64 MiB of HBM per device.

```python
import jax
import jax.numpy as jnp

ROOT = 16384
CHILD = 8192
LEAF = 4096
SOURCES = 128


def levels(key, dims, cuts, smallest, high):
    def one(dim, parts):
        heights = jax.random.uniform(jax.random.fold_in(jax.random.fold_in(key, 6), dim), (parts,), jnp.float32, smallest / len(cuts), high / len(cuts))
        return jnp.repeat(jnp.exp(heights), dims[dim] // parts).reshape((-1,) + (1,) * (len(dims) - dim - 1))

    level = one(*cuts[0])
    for cut in cuts[1:]:
        level = level * one(*cut)
    return level


def centred(own_key, extent, width, reach, cuts=(), kind=jnp.bfloat16):
    factor_of = levels(own_key, extent, cuts, -0.22, 0.18) if cuts else 1.0
    drawn = jax.random.normal(own_key, extent, jnp.float32) * width * factor_of
    return jnp.minimum(jnp.maximum(drawn, -reach), reach).astype(kind)


def setup_inputs(seed: int = 0) -> dict:
    arg_keys = jax.random.split(jax.random.key(seed), 10)
    rhs_root = centred(arg_keys[0], (ROOT, SOURCES), 1.0, 6.0, ((0, 4),), jnp.float32)
    rhs_child = centred(arg_keys[1], (2, CHILD, SOURCES), 1.0, 6.0, ((0, 2), (1, 4)), jnp.float32)
    rhs_leaf = centred(arg_keys[2], (4, LEAF, SOURCES), 1.0, 6.0, ((0, 2), (1, 4)), jnp.float32)
    root_inv = centred(arg_keys[3], (ROOT, ROOT), ROOT ** -0.5, 0.046875, ((0, 32), (1, 4)))
    child_inv = centred(arg_keys[4], (2, CHILD, CHILD), CHILD ** -0.5, 0.0625, ((0, 2), (1, 32), (2, 4)))
    leaf_inv = centred(arg_keys[5], (4, LEAF, LEAF), LEAF ** -0.5, 0.09375, ((0, 2), (1, 32), (2, 4)))
    leaf_to_child = centred(arg_keys[6], (4, CHILD, LEAF), (2 * LEAF) ** -0.5, 0.0625, ((0, 2), (1, 4), (2, 32)))
    leaf_to_root = centred(arg_keys[7], (4, ROOT, LEAF), (2 * CHILD + 4 * LEAF) ** -0.5, 0.03125, ((0, 2), (1, 4), (2, 32)))
    child_to_root = centred(arg_keys[8], (2, ROOT, CHILD), (2 * CHILD + 4 * LEAF) ** -0.5, 0.03125, ((0, 2), (1, 4), (2, 32)))
    return dict(rhs_root=rhs_root, rhs_child=rhs_child, rhs_leaf=rhs_leaf, root_inv=root_inv, child_inv=child_inv, leaf_inv=leaf_inv, leaf_to_child=leaf_to_child, leaf_to_root=leaf_to_root, child_to_root=child_to_root)


def mul(matrix, vector):
    return jnp.dot(matrix, vector.astype(jnp.bfloat16), preferred_element_type=jnp.float32)


def reference(rhs_root, rhs_child, rhs_leaf, root_inv, child_inv, leaf_inv, leaf_to_child, leaf_to_root, child_to_root):
    y_leaf = [mul(leaf_inv[g], rhs_leaf[g]) for g in range(4)]
    y_child = []
    for c in range(2):
        r_child = rhs_child[c] - mul(leaf_to_child[2 * c], y_leaf[2 * c]) - mul(leaf_to_child[2 * c + 1], y_leaf[2 * c + 1])
        y_child.append(mul(child_inv[c], r_child))
    r_root = rhs_root
    for c in range(2):
        r_root = r_root - mul(child_to_root[c], y_child[c])
    for g in range(4):
        r_root = r_root - mul(leaf_to_root[g], y_leaf[g])
    y_root = mul(root_inv, r_root)
    x_root = mul(root_inv.T, y_root)
    x_child = []
    for c in range(2):
        v = y_child[c] - mul(child_to_root[c].T, x_root)
        x_child.append(mul(child_inv[c].T, v))
    x_leaf = []
    for g in range(4):
        v = y_leaf[g] - mul(leaf_to_child[g].T, x_child[g // 2]) - mul(leaf_to_root[g].T, x_root)
        x_leaf.append(mul(leaf_inv[g].T, v))
    return x_root, jnp.stack(x_child), jnp.stack(x_leaf), y_root
```

```python
import jax
import jax.numpy as jnp
from jax import lax
from jax.sharding import Mesh, PartitionSpec as P

F32 = jnp.float32
ROW = ("zh", "zl", "y")
COL = ("xh", "core")
NEAR = ("zl", "y")


def half16(values):
    return values.astype(jnp.bfloat16)


def dot(spec, a, b):
    return jnp.einsum(spec, a, half16(b), preferred_element_type=F32)


def swap(values, axis, size, bit):
    return lax.ppermute(values, axis, [(i, i ^ bit) for i in range(size)])


def scatter(values, axes, count):
    pieces = values.reshape(count, values.shape[0] // count, values.shape[1])
    return lax.all_to_all(pieces, axes, 0, 0).sum(0)


def gather(values, axes, count):
    copies = jnp.broadcast_to(values[None], (count,) + values.shape)
    return lax.all_to_all(copies, axes, 0, 0).reshape(count * values.shape[0], values.shape[1])


def far_sum(values):
    values = values + swap(values, "zh", 4, 1)
    return values + swap(values, "zh", 4, 2)


def row_sum(values):
    return gather(far_sum(scatter(values, NEAR, 8)), NEAR, 8)


def col_sum(values):
    return lax.all_gather(values, COL).sum(0)


def wide_col_sum(values):
    core = lax.axis_index("core")
    rows = values.shape[0] // 2
    low, high = values[:rows], values[rows:]
    mine = jnp.where(core == 0, low, high)
    mine = mine + swap(jnp.where(core == 0, high, low), "core", 2, 1)
    mine = mine + swap(mine, "layer", 2, 1)
    mine = mine + swap(mine, "xh", 2, 1)
    other = swap(mine, "core", 2, 1)
    return jnp.concatenate(
        [jnp.where(core == 0, mine, other), jnp.where(core == 0, other, mine)], axis=0
    )


def on_device(
    rhs_root,
    rhs_child,
    rhs_leaf,
    root_inv,
    child_inv,
    leaf_inv,
    leaf_to_child,
    leaf_to_root,
    child_to_root,
):
    layer = lax.axis_index("layer")
    child_inv, child_to_root = child_inv[0], child_to_root[0]

    y_leaf = dot("gij,gjs->gis", leaf_inv, rhs_leaf)
    y_leaf = col_sum(y_leaf.reshape(-1, 128)).reshape(y_leaf.shape)
    update = dot("gij,gjs->is", leaf_to_child, y_leaf)
    r_child = rhs_child[0] - row_sum(update)
    y_child = col_sum(dot("ij,js->is", child_inv, r_child))
    update = dot("ij,js->is", child_to_root, y_child) + dot("gij,gjs->is", leaf_to_root, y_leaf)

    update = gather(far_sum(scatter(update, ("layer",) + NEAR, 16)), NEAR, 8)
    half = update.shape[0]
    r_root = lax.dynamic_slice_in_dim(rhs_root, layer * half, half) - update
    root_half = lax.dynamic_slice_in_dim(root_inv, layer * half, half, 1)
    y_root = wide_col_sum(dot("ij,js->is", root_half, r_root))
    x_root = far_sum(scatter(dot("ij,is->js", root_half, y_root), NEAR, 8))
    x_root = gather(x_root, ("layer",) + NEAR, 16)

    back_child = y_child - col_sum(dot("ij,is->js", child_to_root, x_root))
    x_child = row_sum(dot("ij,is->js", child_inv, back_child))
    terms = dot("gij,is->gjs", leaf_to_child, x_child) + dot("gij,is->gjs", leaf_to_root, x_root)
    back_leaf = y_leaf - col_sum(terms.reshape(-1, 128)).reshape(y_leaf.shape)
    x_leaf = dot("gij,gis->gjs", leaf_inv, back_leaf)
    x_leaf = row_sum(x_leaf.reshape(-1, 128)).reshape(x_leaf.shape)
    return (x_root, x_child[None], x_leaf, y_root)


def solution(mesh):
    fine = Mesh(
        mesh.devices.reshape(2, 4, 2, 4, 2, 2), ("layer", "zh", "zl", "y", "xh", "core")
    )
    in_specs = (
        P(COL, None),
        P("layer", COL, None),
        P("layer", COL, None),
        P(ROW, COL),
        P("layer", ROW, COL),
        P("layer", ROW, COL),
        P("layer", COL, ROW),
        P("layer", COL, ROW),
        P("layer", COL, ROW),
    )
    out_specs = (P(COL, None), P("layer", COL, None), P("layer", COL, None), P(ROW, None))
    return jax.shard_map(
        on_device, mesh=fine, in_specs=in_specs, out_specs=out_specs, check_vma=False
    )
```

```python
import jax
import jax.numpy as jnp
from jax import lax
from jax.experimental import pallas as pl
from jax.sharding import Mesh, PartitionSpec as P

F32 = jnp.float32
ROW = ("zh", "zl", "y")
COL = ("xh", "core")
NEAR = ("zl", "y")


def half16(values):
    return values.astype(jnp.bfloat16)


def dot(spec, a, b):
    return jnp.einsum(spec, a, half16(b), preferred_element_type=F32)


def swap(values, axis, size, bit):
    return lax.ppermute(values, axis, [(i, i ^ bit) for i in range(size)])


def scatter(values, axes, count):
    pieces = values.reshape(count, values.shape[0] // count, values.shape[1])
    return lax.all_to_all(pieces, axes, 0, 0).sum(0)


def gather(values, axes, count):
    copies = jnp.broadcast_to(values[None], (count,) + values.shape)
    return lax.all_to_all(copies, axes, 0, 0).reshape(count * values.shape[0], values.shape[1])


def paired(values, axes, size, first, second):
    for one, other in ((first, second), (second, first)):
        pairs = []
        for i in range(size):
            pairs.append((2 * i, 2 * (i ^ one)))
            pairs.append((2 * i + 1, 2 * (i ^ other) + 1))
        values = values + lax.ppermute(values, axes + ("core",), pairs)
    return values


def far_sum(values):
    return paired(values, ("zh",), 4, 1, 3)


def row_sum(values, beside=None):
    total = far_sum(scatter(values, NEAR, 8))
    if beside is None:
        return gather(total, NEAR, 8)
    total, beside = lax.optimization_barrier((total, beside))
    return gather(total, NEAR, 8), beside


def col_sum(values):
    values = values + swap(values, "core", 2, 1)
    return values + swap(values, "xh", 2, 1)


def wide_col_sum(values, first):
    rows = values.shape[0] // 2
    low, high = values[:rows], values[rows:]
    mine = jnp.where(first, low, high) + swap(jnp.where(first, high, low), "core", 2, 1)
    mine = paired(mine, ("layer", "xh"), 4, 2, 3)
    other = swap(mine, "core", 2, 1)
    return jnp.concatenate([jnp.where(first, mine, other), jnp.where(first, other, mine)])


def by_group(spec, a, b):
    return [dot(spec, a[g], b[g] if b.ndim == 3 else b) for g in range(a.shape[0])]


def copy_block(from_ref, to_ref):
    to_ref[...] = from_ref[...]


def own_copy(values):
    rows, lanes = values.shape
    block = pl.BlockSpec((rows // 4, lanes), lambda i: (i, 0))
    cost = pl.CostEstimate(flops=0, transcendentals=0, bytes_accessed=8 * rows * lanes)
    return pl.pallas_call(
        copy_block,
        grid=(4,),
        in_specs=[block],
        out_specs=block,
        out_shape=jax.ShapeDtypeStruct(values.shape, values.dtype),
        cost_estimate=cost,
    )(values)


def on_device(
    rhs_root,
    rhs_child,
    rhs_leaf,
    root_inv,
    child_inv,
    leaf_inv,
    leaf_to_child,
    leaf_to_root,
    child_to_root,
):
    child_inv, child_to_root = child_inv[0], child_to_root[0]

    half = rhs_root.shape[0] // 2
    start, first = lax.axis_index("layer") * half, lax.axis_index("core") == 0
    y_leaf = dot("gij,gjs->gis", leaf_inv, rhs_leaf)
    y_leaf, start, first = lax.optimization_barrier((y_leaf, start, first))
    y_leaf = col_sum(y_leaf.reshape(-1, 128)).reshape(2, -1, 128)
    update = sum(by_group("ij,js->is", leaf_to_child, y_leaf))
    leaf_update = sum(by_group("ij,js->is", leaf_to_root, y_leaf))
    update, leaf_update = row_sum(update, leaf_update)
    r_child = rhs_child[0] - update
    y_child = col_sum(dot("ij,js->is", child_inv, r_child))
    update = dot("ij,js->is", child_to_root, y_child) + leaf_update

    update = scatter(update, ("layer",) + NEAR, 16)
    update, start = lax.optimization_barrier((update, start))
    update = far_sum(update)
    rhs_half = lax.dynamic_slice_in_dim(rhs_root, start, half)
    root_half = lax.dynamic_slice_in_dim(root_inv, start, half, 1)
    update, rhs_half, root_half = lax.optimization_barrier((update, rhs_half, root_half))
    r_root = rhs_half - gather(update, NEAR, 8)
    y_root = wide_col_sum(dot("ij,js->is", root_half, r_root), first)
    x_root = far_sum(scatter(dot("ij,is->js", root_half, y_root), NEAR, 8))
    x_root = gather(x_root, ("layer",) + NEAR, 16)

    back_child = y_child - col_sum(dot("ij,is->js", child_to_root, x_root))
    terms = jnp.concatenate(by_group("ij,is->js", leaf_to_root, x_root), axis=0)
    beside = (terms, own_copy(x_root))
    x_child, (terms, x_root) = row_sum(dot("ij,is->js", child_inv, back_child), beside)
    terms = terms + jnp.concatenate(by_group("ij,is->js", leaf_to_child, x_child), axis=0)
    back_leaf = y_leaf - col_sum(terms).reshape(2, -1, 128)
    x_leaf = jnp.concatenate(by_group("ij,is->js", leaf_inv, back_leaf), axis=0)
    x_leaf, x_child = row_sum(x_leaf, own_copy(x_child))
    x_leaf = x_leaf.reshape(2, -1, 128)
    return (x_root, x_child[None], x_leaf, y_root)


def solution(mesh):
    fine = Mesh(
        mesh.devices.reshape(2, 4, 2, 4, 2, 2), ("layer", "zh", "zl", "y", "xh", "core")
    )
    in_specs = (
        P(COL, None),
        P("layer", COL, None),
        P("layer", COL, None),
        P(ROW, COL),
        P("layer", ROW, COL),
        P("layer", ROW, COL),
        P("layer", COL, ROW),
        P("layer", COL, ROW),
        P("layer", COL, ROW),
    )
    out_specs = (P(COL, None), P("layer", COL, None), P("layer", COL, None), P(ROW, None))
    return jax.shard_map(
        on_device, mesh=fine, in_specs=in_specs, out_specs=out_specs, check_vma=False
    )
```

```python
import jax
import jax.numpy as jnp
from jax import lax
from jax.experimental import pallas as pl
from jax.sharding import Mesh, PartitionSpec as P

F32 = jnp.float32
ROW = ("zh", "zl", "y")
COL = ("xh", "core")
NEAR = ("zl", "y")


def half16(values):
    return values.astype(jnp.bfloat16)


def dot(spec, a, b):
    return jnp.einsum(spec, a, half16(b), preferred_element_type=F32)


def swap(values, axis, size, bit):
    return lax.ppermute(values, axis, [(i, i ^ bit) for i in range(size)])


def scatter(values, axes, count):
    pieces = values.reshape(count, values.shape[0] // count, values.shape[1])
    return lax.all_to_all(pieces, axes, 0, 0).sum(0)


def gather(values, axes, count):
    copies = jnp.broadcast_to(values[None], (count,) + values.shape)
    return lax.all_to_all(copies, axes, 0, 0).reshape(count * values.shape[0], values.shape[1])


def paired(values, axes, size, first, second):
    for one, other in ((first, second), (second, first)):
        pairs = []
        for i in range(size):
            pairs.append((2 * i, 2 * (i ^ one)))
            pairs.append((2 * i + 1, 2 * (i ^ other) + 1))
        values = values + lax.ppermute(values, axes + ("core",), pairs)
    return values


def far_sum(values):
    return paired(values, ("zh",), 4, 1, 3)


def row_sum(values, beside=None):
    total = far_sum(scatter(values, NEAR, 8))
    if beside is None:
        return gather(total, NEAR, 8)
    total, beside = lax.optimization_barrier((total, beside))
    return gather(total, NEAR, 8), beside


def col_sum(values):
    values = values + swap(values, "core", 2, 1)
    return values + swap(values, "xh", 2, 1)


def wide_col_sum(values, first):
    rows = values.shape[0] // 2
    low, high = values[:rows], values[rows:]
    mine = jnp.where(first, low, high) + swap(jnp.where(first, high, low), "core", 2, 1)
    far, side, near = [swap(mine, ("layer", "xh"), 4, bit) for bit in (1, 3, 2)]
    mine = (mine + near) + (side + far)
    other = swap(mine, "core", 2, 1)
    return jnp.concatenate([jnp.where(first, mine, other), jnp.where(first, other, mine)])


def by_group(spec, a, b):
    return [dot(spec, a[g], b[g] if b.ndim == 3 else b) for g in range(a.shape[0])]


def copy_block(from_ref, to_ref):
    to_ref[...] = from_ref[...]


def own_copy(values):
    rows, lanes = values.shape
    block = pl.BlockSpec((rows // 4, lanes), lambda i: (i, 0))
    cost = pl.CostEstimate(flops=0, transcendentals=0, bytes_accessed=8 * rows * lanes)
    return pl.pallas_call(
        copy_block,
        grid=(4,),
        in_specs=[block],
        out_specs=block,
        out_shape=jax.ShapeDtypeStruct(values.shape, values.dtype),
        cost_estimate=cost,
    )(values)


def on_device(
    rhs_root,
    rhs_child,
    rhs_leaf,
    root_inv,
    child_inv,
    leaf_inv,
    leaf_to_child,
    leaf_to_root,
    child_to_root,
):
    child_inv, child_to_root = child_inv[0], child_to_root[0]

    half = rhs_root.shape[0] // 2
    start, first = lax.axis_index("layer") * half, lax.axis_index("core") == 0
    y_leaf = dot("gij,gjs->gis", leaf_inv, rhs_leaf)
    y_leaf, start, first = lax.optimization_barrier((y_leaf, start, first))
    y_leaf = col_sum(y_leaf.reshape(-1, 128)).reshape(2, -1, 128)
    update = sum(by_group("ij,js->is", leaf_to_child, y_leaf))
    leaf_update = sum(by_group("ij,js->is", leaf_to_root, y_leaf))
    update, leaf_update = row_sum(update, leaf_update)
    r_child = rhs_child[0] - update
    y_child = col_sum(dot("ij,js->is", child_inv, r_child))
    update = dot("ij,js->is", child_to_root, y_child) + leaf_update

    update = scatter(update, ("layer",) + NEAR, 16)
    update, start = lax.optimization_barrier((update, start))
    update = far_sum(update)
    rhs_half = lax.dynamic_slice_in_dim(rhs_root, start, half)
    root_half = lax.dynamic_slice_in_dim(root_inv, start, half, 1)
    update, rhs_half, root_half = lax.optimization_barrier((update, rhs_half, root_half))
    r_root = rhs_half - gather(update, NEAR, 8)
    y_root = wide_col_sum(dot("ij,js->is", root_half, r_root), first)
    x_root = far_sum(scatter(dot("ij,is->js", root_half, y_root), NEAR, 8))
    x_root = gather(x_root, ("layer",) + NEAR, 16)

    back_child = y_child - col_sum(dot("ij,is->js", child_to_root, x_root))
    terms = jnp.concatenate(by_group("ij,is->js", leaf_to_root, x_root), axis=0)
    beside = (terms, own_copy(x_root))
    x_child, (terms, x_root) = row_sum(dot("ij,is->js", child_inv, back_child), beside)
    terms = terms + jnp.concatenate(by_group("ij,is->js", leaf_to_child, x_child), axis=0)
    back_leaf = y_leaf - col_sum(terms).reshape(2, -1, 128)
    x_leaf = jnp.concatenate(by_group("ij,is->js", leaf_inv, back_leaf), axis=0)
    x_leaf, x_child = row_sum(x_leaf, own_copy(x_child))
    x_leaf = x_leaf.reshape(2, -1, 128)
    return (x_root, x_child[None], x_leaf, y_root)


def solution(mesh):
    fine = Mesh(
        mesh.devices.reshape(2, 4, 2, 4, 2, 2), ("layer", "zh", "zl", "y", "xh", "core")
    )
    in_specs = (
        P(COL, None),
        P("layer", COL, None),
        P("layer", COL, None),
        P(ROW, COL),
        P("layer", ROW, COL),
        P("layer", ROW, COL),
        P("layer", COL, ROW),
        P("layer", COL, ROW),
        P("layer", COL, ROW),
    )
    out_specs = (P(COL, None), P("layer", COL, None), P("layer", COL, None), P(ROW, None))
    return jax.shard_map(
        on_device, mesh=fine, in_specs=in_specs, out_specs=out_specs, check_vma=False
    )
```

```python
import jax
import jax.numpy as jnp
from jax import lax
from jax.experimental import pallas as pl
from jax.sharding import Mesh, PartitionSpec as P

F32 = jnp.float32
ROW = ("zh", "zl", "y")
COL = ("xh", "core")
NEAR = ("zl", "y")


def half16(values):
    return values.astype(jnp.bfloat16)


def dot(spec, a, b):
    return jnp.einsum(spec, a, half16(b), preferred_element_type=F32)


def swap(values, axis, size, bit):
    return lax.ppermute(values, axis, [(i, i ^ bit) for i in range(size)])


def scatter(values, axes, count):
    pieces = values.reshape(count, values.shape[0] // count, values.shape[1])
    return lax.all_to_all(pieces, axes, 0, 0).sum(0)


def gather(values, axes, count):
    copies = jnp.broadcast_to(values[None], (count,) + values.shape)
    return lax.all_to_all(copies, axes, 0, 0).reshape(count * values.shape[0], values.shape[1])


def paired(values, axes, size, first, second):
    for one, other in ((first, second), (second, first)):
        pairs = []
        for i in range(size):
            pairs.append((2 * i, 2 * (i ^ one)))
            pairs.append((2 * i + 1, 2 * (i ^ other) + 1))
        values = values + lax.ppermute(values, axes + ("core",), pairs)
    return values


def far_sum(values):
    return paired(values, ("zh",), 4, 1, 3)


def row_sum(values, beside=None):
    total = far_sum(scatter(values, NEAR, 8))
    if beside is None:
        return gather(total, NEAR, 8)
    total, beside = lax.optimization_barrier((total, beside))
    return gather(total, NEAR, 8), beside


def col_sum(values):
    values = values + swap(values, "core", 2, 1)
    return values + swap(values, "xh", 2, 1)


def wide_col_sum(values, first):
    rows = values.shape[0] // 2
    low, high = values[:rows], values[rows:]
    mine = jnp.where(first, low, high) + swap(jnp.where(first, high, low), "core", 2, 1)
    far, side, near = [swap(mine, ("layer", "xh"), 4, bit) for bit in (1, 3, 2)]
    mine = (mine + near) + (side + far)
    other = swap(mine, "core", 2, 1)
    return jnp.concatenate([jnp.where(first, mine, other), jnp.where(first, other, mine)])


def by_group(spec, a, b):
    return [dot(spec, a[g], b[g] if b.ndim == 3 else b) for g in range(a.shape[0])]


def copy_block(from_ref, to_ref):
    to_ref[...] = from_ref[...]


def own_copy(values):
    rows, lanes = values.shape
    block = pl.BlockSpec((rows // 4, lanes), lambda i: (i, 0))
    cost = pl.CostEstimate(flops=0, transcendentals=0, bytes_accessed=8 * rows * lanes)
    return pl.pallas_call(
        copy_block,
        grid=(4,),
        in_specs=[block],
        out_specs=block,
        out_shape=jax.ShapeDtypeStruct(values.shape, values.dtype),
        cost_estimate=cost,
    )(values)


def on_device(
    rhs_root,
    rhs_child,
    rhs_leaf,
    root_inv,
    child_inv,
    leaf_inv,
    leaf_to_child,
    leaf_to_root,
    child_to_root,
):
    child_inv, child_to_root = child_inv[0], child_to_root[0]

    half = rhs_root.shape[0] // 2
    start, first = lax.axis_index("layer") * half, lax.axis_index("core") == 0
    y_leaf = dot("gij,gjs->gis", leaf_inv, rhs_leaf)
    y_leaf, start, first = lax.optimization_barrier((y_leaf, start, first))
    y_leaf = col_sum(y_leaf.reshape(-1, 128)).reshape(2, -1, 128)
    update = sum(by_group("ij,js->is", leaf_to_child, y_leaf))
    leaf_update = sum(by_group("ij,js->is", leaf_to_root, y_leaf))
    update, leaf_update = row_sum(update, leaf_update)
    r_child = rhs_child[0] - update
    y_child = col_sum(dot("ij,js->is", child_inv, r_child))
    update = dot("ij,js->is", child_to_root, y_child) + leaf_update

    update = scatter(update, ("layer",) + NEAR, 16)
    update, start = lax.optimization_barrier((update, start))
    update = far_sum(update)
    rhs_half = lax.dynamic_slice_in_dim(rhs_root, start, half)
    root_half = lax.dynamic_slice_in_dim(root_inv, start, half, 1)
    update, rhs_half, root_half = lax.optimization_barrier((update, rhs_half, root_half))
    r_root = rhs_half - gather(update, NEAR, 8)
    y_root = wide_col_sum(dot("ij,js->is", root_half, r_root), first)
    x_root = far_sum(scatter(dot("ij,is->js", root_half, y_root), NEAR, 8))
    x_root = gather(x_root, ("layer",) + NEAR, 16)

    back = dot("ij,is->js", child_to_root, x_root)
    back = back + swap(back, "core", 2, 1)
    back, solved = lax.optimization_barrier((back, x_root))
    solved = own_copy(solved)
    back = back + swap(back, "xh", 2, 1)
    back, solved = lax.optimization_barrier((back, solved))
    back_child = y_child - back
    terms = jnp.concatenate(by_group("ij,is->js", leaf_to_root, x_root), axis=0)
    x_child, terms = row_sum(dot("ij,is->js", child_inv, back_child), terms)
    terms = terms + jnp.concatenate(by_group("ij,is->js", leaf_to_child, x_child), axis=0)
    back_leaf = y_leaf - col_sum(terms).reshape(2, -1, 128)
    x_leaf = jnp.concatenate(by_group("ij,is->js", leaf_inv, back_leaf), axis=0)
    x_leaf, x_child = row_sum(x_leaf, own_copy(x_child))
    x_leaf = x_leaf.reshape(2, -1, 128)
    return (solved, x_child[None], x_leaf, y_root)


def solution(mesh):
    fine = Mesh(
        mesh.devices.reshape(2, 4, 2, 4, 2, 2), ("layer", "zh", "zl", "y", "xh", "core")
    )
    in_specs = (
        P(COL, None),
        P("layer", COL, None),
        P("layer", COL, None),
        P(ROW, COL),
        P("layer", ROW, COL),
        P("layer", ROW, COL),
        P("layer", COL, ROW),
        P("layer", COL, ROW),
        P("layer", COL, ROW),
    )
    out_specs = (P(COL, None), P("layer", COL, None), P("layer", COL, None), P(ROW, None))
    return jax.shard_map(
        on_device, mesh=fine, in_specs=in_specs, out_specs=out_specs, check_vma=False
    )
```

```python
import jax
import jax.numpy as jnp
from jax import lax
from jax.experimental import pallas as pl
from jax.sharding import Mesh, PartitionSpec as P

F32 = jnp.float32
ROW = ("zh", "zl", "y")
COL = ("xh", "core")
NEAR = ("zl", "y")


def half16(values):
    return values.astype(jnp.bfloat16)


def dot(spec, a, b):
    return jnp.einsum(spec, a, half16(b), preferred_element_type=F32)


def swap(values, axis, size, bit):
    return lax.ppermute(values, axis, [(i, i ^ bit) for i in range(size)])


def scatter(values, axes, count):
    pieces = values.reshape(count, values.shape[0] // count, values.shape[1])
    return lax.all_to_all(pieces, axes, 0, 0).sum(0)


def gather(values, axes, count):
    copies = jnp.broadcast_to(values[None], (count,) + values.shape)
    return lax.all_to_all(copies, axes, 0, 0).reshape(count * values.shape[0], values.shape[1])


def paired(values, axes, size, first, second):
    for one, other in ((first, second), (second, first)):
        pairs = []
        for i in range(size):
            pairs.append((2 * i, 2 * (i ^ one)))
            pairs.append((2 * i + 1, 2 * (i ^ other) + 1))
        values = values + lax.ppermute(values, axes + ("core",), pairs)
    return values


def far_sum(values):
    return paired(values, ("zh",), 4, 1, 3)


def row_sum(values, beside=None):
    total = far_sum(scatter(values, NEAR, 8))
    if beside is None:
        return gather(total, NEAR, 8)
    total, beside = lax.optimization_barrier((total, beside))
    return gather(total, NEAR, 8), beside


def col_sum(values):
    values = values + swap(values, "core", 2, 1)
    return values + swap(values, "xh", 2, 1)


def wide_col_sum(values, first):
    rows = values.shape[0] // 2
    low, high = values[:rows], values[rows:]
    mine = jnp.where(first, low, high) + swap(jnp.where(first, high, low), "core", 2, 1)
    far, side, near = [swap(mine, ("layer", "xh"), 4, bit) for bit in (1, 3, 2)]
    mine = (mine + near) + (side + far)
    other = swap(mine, "core", 2, 1)
    return jnp.concatenate([jnp.where(first, mine, other), jnp.where(first, other, mine)])


def by_group(spec, a, b):
    return [dot(spec, a[g], b[g] if b.ndim == 3 else b) for g in range(a.shape[0])]


def copy_block(from_ref, to_ref):
    to_ref[...] = from_ref[...]


def own_copy(values):
    rows, lanes = values.shape
    block = pl.BlockSpec((rows // 4, lanes), lambda i: (i, 0))
    cost = pl.CostEstimate(flops=0, transcendentals=0, bytes_accessed=8 * rows * lanes)
    return pl.pallas_call(
        copy_block,
        grid=(4,),
        in_specs=[block],
        out_specs=block,
        out_shape=jax.ShapeDtypeStruct(values.shape, values.dtype),
        cost_estimate=cost,
    )(values)


def on_device(
    rhs_root,
    rhs_child,
    rhs_leaf,
    root_inv,
    child_inv,
    leaf_inv,
    leaf_to_child,
    leaf_to_root,
    child_to_root,
):
    child_inv, child_to_root = child_inv[0], child_to_root[0]

    half = rhs_root.shape[0] // 2
    start, first = lax.axis_index("layer") * half, lax.axis_index("core") == 0
    y_leaf = dot("gij,gjs->gis", leaf_inv, rhs_leaf)
    y_leaf, start, first = lax.optimization_barrier((y_leaf, start, first))
    y_leaf = col_sum(y_leaf.reshape(-1, 128)).reshape(2, -1, 128)
    update = sum(by_group("ij,js->is", leaf_to_child, y_leaf))
    leaf_update = sum(by_group("ij,js->is", leaf_to_root, y_leaf))
    update, leaf_update = row_sum(update, leaf_update)
    r_child = rhs_child[0] - update
    y_child = col_sum(dot("ij,js->is", child_inv, r_child))
    update = dot("ij,js->is", child_to_root, y_child) + leaf_update

    update = scatter(update, ("layer",) + NEAR, 16)
    update, start = lax.optimization_barrier((update, start))
    update = far_sum(update)
    rhs_half = lax.dynamic_slice_in_dim(rhs_root, start, half)
    root_half = lax.dynamic_slice_in_dim(root_inv, start, half, 1)
    update, rhs_half, root_half = lax.optimization_barrier((update, rhs_half, root_half))
    r_root = rhs_half - gather(update, NEAR, 8)
    y_root = wide_col_sum(dot("ij,js->is", root_half, r_root), first)
    x_root = far_sum(scatter(dot("ij,is->js", root_half, y_root), NEAR, 8))
    x_root = gather(x_root, ("layer",) + NEAR, 16)

    back = dot("ij,is->js", child_to_root, x_root)
    back = back + swap(back, "core", 2, 1)
    back, solved = lax.optimization_barrier((back, x_root))
    solved = own_copy(solved)
    back = back + swap(back, "xh", 2, 1)
    back, solved = lax.optimization_barrier((back, solved))
    back_child = y_child - back
    terms = jnp.concatenate(by_group("ij,is->js", leaf_to_root, x_root), axis=0)
    x_child, terms = row_sum(dot("ij,is->js", child_inv, back_child), terms)
    terms = terms + jnp.concatenate(by_group("ij,is->js", leaf_to_child, x_child), axis=0)
    terms = terms + swap(terms, "core", 2, 1)
    terms, x_child = lax.optimization_barrier((terms, x_child))
    x_child = own_copy(x_child)
    terms = terms + swap(terms, "xh", 2, 1)
    terms, x_child = lax.optimization_barrier((terms, x_child))
    back_leaf = y_leaf - terms.reshape(2, -1, 128)
    x_leaf = jnp.concatenate(by_group("ij,is->js", leaf_inv, back_leaf), axis=0)
    x_leaf = row_sum(x_leaf).reshape(2, -1, 128)
    return (solved, x_child[None], x_leaf, y_root)


def solution(mesh):
    fine = Mesh(
        mesh.devices.reshape(2, 4, 2, 4, 2, 2), ("layer", "zh", "zl", "y", "xh", "core")
    )
    in_specs = (
        P(COL, None),
        P("layer", COL, None),
        P("layer", COL, None),
        P(ROW, COL),
        P("layer", ROW, COL),
        P("layer", ROW, COL),
        P("layer", COL, ROW),
        P("layer", COL, ROW),
        P("layer", COL, ROW),
    )
    out_specs = (P(COL, None), P("layer", COL, None), P("layer", COL, None), P(ROW, None))
    return jax.shard_map(
        on_device, mesh=fine, in_specs=in_specs, out_specs=out_specs, check_vma=False
    )
```
